32 devices in a mesh: groups: 2 (over y), frames: 4 (over z), rows: 2 (over x), heads: 2 (over core).
Axes of the slice: x: 2, y: 2, z: 4, core: 2. Of those that a mesh axis runs over, the one named last changes fastest.
Arguments:
- clip_latent: bfloat16 [8, 12, 48, 640], P(('groups', 'frames'), 'rows', None, 'heads'), parts along dimension 0, may hold values from -40 to 40, as said below
- norm_gain: float32 [640], replicated, may hold values from 0.1 to 1.9
- w_time: bfloat16 [3, 640, 640], replicated, may hold values from -0.125 to 0.125
- w_query: bfloat16 [640, 640], P(None, 'heads'), may hold values from -0.7109375 to 0.7109375
- w_key: bfloat16 [640, 640], P(None, 'heads'), may hold values from -0.25 to 0.25
- w_value: bfloat16 [640, 640], P(None, 'heads'), may hold values from -0.25 to 0.25
- w_out: bfloat16 [640, 640], P('heads'), may hold values from -0.25 to 0.25
- reference_tokens: bfloat16 [288, 640], P(('groups', 'frames', 'rows'), 'heads'), parts along dimension 0, may hold values from -160 to 160, as said below
Outputs:
- block_out: bfloat16 [8, 12, 48, 640], P(('groups', 'frames'), 'rows', None, 'heads'), parts along dimension 0
The draws below stay inside these ranges and needn't reach their ends.
There are 2 independent parts, one for each index of `groups`. The reference program is written for one: setup_inputs(seed, part) draws one part's arguments, and reference() takes and returns one part's arrays. A program takes and returns all parts, laid end to end along the dimension named above; an argument that names none is the same for every part. Nothing has to cross between parts.
Inputs may be any that keep to these rules, and one draw needn't show every extreme that they name: `clip_latent`: Real-valued latent features; each channel and each position has its own scale. `reference_tokens`: Real-valued reference features.
All inputs are finite; a program needn't handle non-finite values.
Results may differ from the reference program's by a relative error of at most 0.022.
Values may be sent and summed in bfloat16 or wider, within the bound.
A program may use at most 64 MiB of HBM per device.

```python
import math
import jax
import jax.numpy as jnp
from jax import lax

C = 640
HEADS = 8
FRAMES = 4
LH = 12
LW = 48
RT = 144


def draw_clip_latent(key, part):
    keys = jax.random.split(jax.random.fold_in(key, 11), 3)
    chan_scale = jnp.exp(jax.random.uniform(keys[0], (C,), jnp.float32, 0.0, math.log(3.2)))
    tok_scale = jnp.exp(jax.random.uniform(keys[1], (FRAMES, LH, LW, 1), jnp.float32, 0.0, math.log(3.2)))
    base = jax.random.normal(keys[2], (FRAMES, LH, LW, C), jnp.float32)
    return jnp.clip(base * chan_scale * tok_scale, -40.0, 40.0).astype(jnp.bfloat16)


def draw_reference_tokens(key, part):
    keys = jax.random.split(jax.random.fold_in(key, 23), 3)
    base = jax.random.normal(keys[2], (RT, C), jnp.float32)
    return jnp.clip(base, -6.0, 6.0).astype(jnp.bfloat16)


def steps_of(key, shape, cuts, least, top_value):
    def one(dim, blocks):
        heights = jax.random.uniform(jax.random.fold_in(jax.random.fold_in(key, 6), dim), (blocks,), jnp.float32, least / len(cuts), top_value / len(cuts))
        return jnp.repeat(jnp.exp(heights), shape[dim] // blocks).reshape((-1,) + (1,) * (len(shape) - dim - 1))

    loudness = one(*cuts[0])
    for cut in cuts[1:]:
        loudness = loudness * one(*cut)
    return loudness


def bell_draw(rng, shape, scale, limit, shards=(), kind=jnp.bfloat16):
    entries = scale * jax.random.normal(rng, shape, jnp.float32)
    if shards:
        entries = entries * steps_of(rng, shape, shards, -0.22, 0.18)
    return jnp.clip(entries, -limit, limit).astype(kind)


def setup_inputs(seed: int = 0, part: int = 0) -> dict:
    key_list = jax.random.split(jax.random.key(seed), 9)
    own_keys = jax.random.split(jax.random.fold_in(key_list[8], part), 9)
    clip_latent = draw_clip_latent(jax.random.fold_in(jax.random.fold_in(key_list[8], part), 71), part)
    norm_gain = jnp.clip(1.0 + 0.18 * jax.random.normal(key_list[1], (C,), jnp.float32), 0.1, 1.9)
    w_time = bell_draw(key_list[2], (3, C, C), (3 * C) ** -0.5, 0.125)
    w_query = bell_draw(key_list[3], (C, C), (3.0 * C ** -0.5), 0.7109375, ((1, 2),))
    w_key = bell_draw(key_list[4], (C, C), C ** -0.5, 0.25, ((1, 2),))
    w_value = bell_draw(key_list[5], (C, C), C ** -0.5, 0.25, ((1, 2),))
    w_out = bell_draw(key_list[6], (C, C), C ** -0.5, 0.25, ((0, 2),))
    reference_tokens = draw_reference_tokens(jax.random.fold_in(jax.random.fold_in(key_list[8], part), 71), part)
    return dict(clip_latent=clip_latent, norm_gain=norm_gain, w_time=w_time, w_query=w_query, w_key=w_key, w_value=w_value, w_out=w_out, reference_tokens=reference_tokens)


def attend_head(operands):
    query_head, key_head, value_head = operands
    scores = jnp.dot(query_head, key_head.T, preferred_element_type=jnp.float32)
    top = lax.optimization_barrier(jnp.max(scores, axis=1, keepdims=True))
    expo = jnp.exp(scores - top)
    total = lax.optimization_barrier(jnp.sum(expo, axis=1, keepdims=True))
    probs = expo.astype(jnp.bfloat16)
    return (jnp.dot(probs, value_head, preferred_element_type=jnp.float32) / total).astype(jnp.bfloat16)

def reference(clip_latent, norm_gain, w_time, w_query, w_key, w_value, w_out, reference_tokens):
    frames_all = clip_latent.shape[0]
    head_size = C // HEADS
    padded = jnp.pad(clip_latent, ((1, 1), (0, 0), (0, 0), (0, 0)))
    summed = jnp.dot(padded[0:frames_all], w_time[0], preferred_element_type=jnp.float32)
    summed = summed + jnp.dot(padded[1:1 + frames_all], w_time[1], preferred_element_type=jnp.float32)
    summed = summed + jnp.dot(padded[2:2 + frames_all], w_time[2], preferred_element_type=jnp.float32)
    temporal = (clip_latent.astype(jnp.float32) + summed).astype(jnp.bfloat16)
    feats = temporal.astype(jnp.float32)
    centre = lax.optimization_barrier(jnp.mean(feats, axis=-1, keepdims=True))
    spread = lax.optimization_barrier(jnp.mean((feats - centre) ** 2, axis=-1, keepdims=True))
    normed = ((feats - centre) * lax.rsqrt(spread + 1e-05) * norm_gain).astype(jnp.bfloat16)
    scale = 1.0 / jnp.sqrt(jnp.float32(head_size))
    query = (jnp.dot(normed, w_query, preferred_element_type=jnp.float32) * scale).astype(jnp.bfloat16)
    keys = jnp.dot(reference_tokens, w_key, preferred_element_type=jnp.float32).astype(jnp.bfloat16)
    values = jnp.dot(reference_tokens, w_value, preferred_element_type=jnp.float32).astype(jnp.bfloat16)
    key_heads = keys.reshape(-1, HEADS, head_size).transpose(1, 0, 2)
    value_heads = values.reshape(-1, HEADS, head_size).transpose(1, 0, 2)

    def per_frame(query_frame):
        rows_here, cols_here, chans = query_frame.shape
        query_heads = query_frame.reshape(-1, HEADS, head_size).transpose(1, 0, 2)
        result = lax.map(attend_head, (query_heads, key_heads, value_heads))
        return result.transpose(1, 0, 2).reshape(rows_here, cols_here, chans)
    attended = lax.map(per_frame, query)
    mixed = jnp.dot(attended, w_out, preferred_element_type=jnp.float32)
    return (temporal.astype(jnp.float32) + mixed).astype(jnp.bfloat16)
```

```python
import functools

import jax
import jax.numpy as jnp
from jax import lax
from jax.experimental import pallas as pl
from jax.experimental.pallas import tpu as pltpu
from jax.sharding import PartitionSpec as P

HEAD_SIZE = 80
BF16 = jnp.bfloat16
F32 = jnp.float32
MESH = pl.DeviceIdType.MESH


def dot(a, b):
    return jnp.dot(a, b, preferred_element_type=F32)


def kernel(
    sizes,
    clip, gain, w_time, w_query, w_key, w_value, w_out, tokens,
    out,
    x, wt, wq, wk, wv, wo, wo_half, gains, slots, tok, keys, values, base, att,
    local_sem, halo_send, halo_recv, relay_send, relay_recv, pair_send, pair_recv,
    near_send, near_recv, far_send, far_recv, att_send, att_recv,
):
    nf, nr, nh, chunks, pad = sizes
    positions, half = clip.shape
    count = tokens.shape[0]
    local_heads = half // HEAD_SIZE
    step = positions // chunks
    f, r, h = lax.axis_index("frames"), lax.axis_index("rows"), lax.axis_index("heads")
    other = 1 - h
    partner = {"heads": other}

    def remote(src, dst, send, recv, to):
        return pltpu.make_async_remote_copy(
            src_ref=src, dst_ref=dst, send_sem=send, recv_sem=recv, device_id=to, device_id_type=MESH
        )

    def rows_of(c):
        return pl.ds(c * step, step)

    barrier = pltpu.get_barrier_semaphore()
    plane = [(a, b) for a in range(nr) for b in range(nh) if (a, b) != (0, 0)]

    def plane_to(a, b):
        return {"rows": lax.rem(r + a, nr), "heads": lax.rem(h + b, nh)}

    for a, b in plane:
        pl.semaphore_signal(barrier, inc=1, device_id=plane_to(a, b), device_id_type=MESH)
    for d in range(1, nf):
        pl.semaphore_signal(barrier, inc=1, device_id={"frames": lax.rem(f + d, nf)}, device_id_type=MESH)

    mine = r * nf + f
    loads = [
        pltpu.make_async_copy(src, dst, local_sem.at[i])
        for i, (src, dst) in enumerate(
            [
                (tokens, slots.at[h, mine]),
                (clip, x.at[1, h]),
                (w_time, wt),
                (w_out, wo.at[0]),
                (w_key, wk),
                (w_value, wv),
                (w_query, wq),
                (gain, gains),
            ]
        )
    ]
    for load in loads:
        load.start()

    tok[...] = jnp.zeros_like(tok)

    @pl.when(f == 0)
    def _():
        x[0] = jnp.zeros(x.shape[1:], BF16)

    @pl.when(f == nf - 1)
    def _():
        x[2] = jnp.zeros(x.shape[1:], BF16)

    pl.semaphore_wait(barrier, len(plane) + nf - 1)

    near = [
        remote(tokens, slots.at[h, mine], near_send.at[d], near_recv.at[d], {"frames": lax.rem(f + d, nf)})
        for d in range(1, nf)
    ]
    for copy in near:
        copy.start()

    def halo(side, c):
        to = f + 1 if side == 0 else f - 1
        slot = 0 if side == 0 else 2
        return remote(
            clip.at[rows_of(c)], x.at[slot, h, rows_of(c)], halo_send.at[side, c], halo_recv.at[side, c],
            {"frames": to},
        )

    def relay(side, c):
        slot = 0 if side == 0 else 2
        ref = x.at[slot, h, rows_of(c)]
        return remote(ref, ref, relay_send.at[side, c], relay_recv.at[side, c], partner)

    sends = (f < nf - 1, f > 0)
    gets = (f > 0, f < nf - 1)
    for c in range(chunks):
        for side in range(2):
            @pl.when(sends[side])
            def _():
                halo(side, c).start()

    pair = [
        remote(clip, x.at[1, h], pair_send.at[0], pair_recv.at[0], partner),
        remote(w_out, wo.at[1], pair_send.at[1], pair_recv.at[1], partner),
    ]
    for copy in pair:
        copy.start()

    def weight(o, which):
        return wt[o, pl.ds(pl.multiple_of(which * half, half), half), :]

    loads[1].wait()
    loads[2].wait()
    pair[0].wait_recv()
    first = jnp.concatenate([x[1, 0].astype(F32), x[1, 1].astype(F32)], axis=1)
    base[...] = first + dot(x[1, 0], wt[1, :half, :]) + dot(x[1, 1], wt[1, half:, :])

    loads[3].wait()
    pair[1].wait_recv()
    for k in range(2):
        whole = wo[k].astype(F32)
        wo_half[k] = jnp.where(h == 0, whole[:, :half], whole[:, half:]).astype(BF16)

    loads[0].wait()
    for copy in near:
        copy.wait_recv()
    line = slots.at[h, pl.ds(r * nf, nf)]
    far = [remote(line, line, far_send.at[a, b], far_recv.at[a, b], plane_to(a, b)) for a, b in plane]
    for copy in far:
        copy.start()

    def arrive(c):
        for side in range(2):
            @pl.when(gets[side])
            def _():
                halo(side, c).wait_recv()
                relay(side, c).start()
        rows = rows_of(c)
        base[rows] = base[rows] + dot(x[0, h, rows], weight(0, h)) + dot(x[2, h, rows], weight(2, h))

    def make_keys():
        for copy in far:
            copy.wait_recv()
        for k in range(nh):
            if nr * nf <= 16:
                for i in range(nr * nf):
                    tok[k, pl.ds(i * pad, count), :] = slots[k, i]
            else:
                def place(i, carry):
                    tok[k, pl.ds(pl.multiple_of(i * pad, pad), count), :] = slots[k, i]
                    return carry

                lax.fori_loop(0, nr * nf, place, 0)
        loads[4].wait()
        loads[5].wait()
        block = min(256, tok.shape[1])

        def project(i, carry):
            at = pl.ds(pl.multiple_of(i * block, block), block)
            head = lax.broadcasted_iota(jnp.int32, (block, half), 1)
            for weights, dest in ((wk, keys), (wv, values)):
                full = dot(tok[0, at, :], weights[:half, :]) + dot(tok[1, at, :], weights[half:, :])
                for k in range(local_heads):
                    inside = (head >= k * HEAD_SIZE) & (head < (k + 1) * HEAD_SIZE)
                    dest[k, at, :] = jnp.where(inside, full, 0.0).astype(BF16)
            return carry

        trips = tok.shape[1] // block
        if trips == 1:
            project(0, 0)
        else:
            lax.fori_loop(0, trips, project, 0)
        loads[6].wait()
        loads[7].wait()

    scale = 1.0 / (HEAD_SIZE ** 0.5)

    def attended(c):
        return remote(att.at[0, rows_of(c)], att.at[1, rows_of(c)], att_send.at[c], att_recv.at[c], partner)

    def process(c):
        rows = rows_of(c)
        for side in range(2):
            @pl.when(gets[side])
            def _():
                relay(side, c).wait_recv()
        summed = base[rows] + dot(x[0, other, rows], weight(0, other)) + dot(x[2, other, rows], weight(2, other))
        feats = summed.astype(BF16).astype(F32)
        base[rows] = feats
        centre = jnp.mean(feats, axis=-1, keepdims=True)
        moved = feats - centre
        spread = jnp.mean(moved * moved, axis=-1, keepdims=True)
        normed = (moved * lax.rsqrt(spread + 1e-05) * gains[...]).astype(BF16)
        query = (dot(normed, wq[...]) * scale).astype(BF16)
        total_tokens = tok.shape[1]
        column = lax.broadcasted_iota(jnp.int32, (step, total_tokens), 1)
        valid = lax.rem(column, pad) < count
        result = jnp.zeros((step, half), F32)
        for k in range(local_heads):
            scores = lax.dot_general(query, keys[k], (((1,), (1,)), ((), ())), preferred_element_type=F32)
            scores = jnp.where(valid, scores, -3e38)
            expo = jnp.exp(scores - jnp.max(scores, axis=1, keepdims=True))
            total = jnp.sum(expo, axis=1, keepdims=True)
            result = result + dot(expo.astype(BF16), values[k]) * (1.0 / total)
        att[0, rows] = result.astype(BF16)
        attended(c).start()

    def finish(c):
        rows = rows_of(c)
        feats = base[rows]
        own = jnp.where(h == 0, feats[:, :half], feats[:, half:])
        mixed = own + dot(att[0, rows], wo_half[0])
        attended(c).wait_recv()
        out[rows] = (mixed + dot(att[1, rows], wo_half[1])).astype(BF16)

    arrive(0)
    for c in range(1, min(2, chunks)):
        arrive(c)
    make_keys()
    for c in range(chunks):
        process(c)
        if c + 2 < chunks:
            arrive(c + 2)
        if c >= 1:
            finish(c - 1)
    finish(chunks - 1)

    for copy in near + pair + far:
        copy.wait_send()
    for c in range(chunks):
        attended(c).wait_send()
        for side in range(2):
            @pl.when(sends[side])
            def _():
                halo(side, c).wait_send()

            @pl.when(gets[side])
            def _():
                relay(side, c).wait_send()


def body(sizes, clip_latent, norm_gain, w_time, w_query, w_key, w_value, w_out, reference_tokens):
    nf, nr, nh = sizes
    shape = clip_latent.shape
    half, width = w_out.shape
    positions = shape[0] * shape[1] * shape[2]
    assert shape[0] == 1 and nh == 2
    chunks = next(n for n in (3, 2, 1) if positions % (16 * n) == 0)
    count = reference_tokens.shape[0]
    pad = -(-count // 16) * 16
    total = pad * nf * nr
    heads = half // HEAD_SIZE
    dma = pltpu.SemaphoreType.DMA
    result = pl.pallas_call(
        functools.partial(kernel, (nf, nr, nh, chunks, pad)),
        out_shape=jax.ShapeDtypeStruct((positions, half), BF16),
        in_specs=[pl.BlockSpec(memory_space=pl.ANY)] * 8,
        out_specs=pl.BlockSpec(memory_space=pltpu.VMEM),
        scratch_shapes=[
            pltpu.VMEM((3, 2, positions, half), BF16),
            pltpu.VMEM(w_time.shape, BF16),
            pltpu.VMEM(w_query.shape, BF16),
            pltpu.VMEM(w_key.shape, BF16),
            pltpu.VMEM(w_value.shape, BF16),
            pltpu.VMEM((2, half, width), BF16),
            pltpu.VMEM((2, half, half), BF16),
            pltpu.VMEM((1, width), F32),
            pltpu.VMEM((nh, nr * nf, count, half), BF16),
            pltpu.VMEM((nh, total, half), BF16),
            pltpu.VMEM((heads, total, half), BF16),
            pltpu.VMEM((heads, total, half), BF16),
            pltpu.VMEM((positions, width), F32),
            pltpu.VMEM((2, positions, half), BF16),
            dma((8,)),
            dma((2, chunks)),
            dma((2, chunks)),
            dma((2, chunks)),
            dma((2, chunks)),
            dma((2,)),
            dma((2,)),
            dma((nf,)),
            dma((nf,)),
            dma((nr, nh)),
            dma((nr, nh)),
            dma((chunks,)),
            dma((chunks,)),
        ],
        compiler_params=pltpu.CompilerParams(collective_id=0, has_side_effects=True),
    )(
        clip_latent.reshape(positions, half),
        norm_gain.reshape(1, width),
        w_time, w_query, w_key, w_value, w_out, reference_tokens,
    )
    return result.reshape(shape)


def solution(mesh):
    sizes = (mesh.shape["frames"], mesh.shape["rows"], mesh.shape["heads"])
    return jax.shard_map(
        functools.partial(body, sizes),
        mesh=mesh,
        in_specs=(
            P(("groups", "frames"), "rows", None, "heads"),
            P(),
            P(),
            P(None, "heads"),
            P(None, "heads"),
            P(None, "heads"),
            P("heads", None),
            P(("groups", "frames", "rows"), "heads"),
        ),
        out_specs=P(("groups", "frames"), "rows", None, "heads"),
        check_vma=False,
    )
```

```python
import functools

import jax
import jax.numpy as jnp
from jax import lax
from jax.experimental import pallas as pl
from jax.experimental.pallas import tpu as pltpu
from jax.sharding import PartitionSpec as P

HEAD_SIZE = 80
BF16 = jnp.bfloat16
F32 = jnp.float32
MESH = pl.DeviceIdType.MESH


def dot_t(a, b):
    return lax.dot_general(a, b, (((1,), (1,)), ((), ())), preferred_element_type=F32)


def dot(a, b):
    return jnp.dot(a, b, preferred_element_type=F32)


def kernel(
    sizes,
    clip, gain, w_time, w_query, w_key, w_value, w_out, tokens,
    out,
    x, wt, wq, wk, wv, wo, wo_half, gains, slots, tok, keys, values, base, att,
    local_sem, halo_send, halo_recv, relay_send, relay_recv, pair_send, pair_recv,
    near_send, near_recv, far_send, far_recv, att_send, att_recv,
):
    nf, nr, nh, chunks, pad = sizes
    positions, half = clip.shape
    count = tokens.shape[0]
    local_heads = half // HEAD_SIZE
    step = positions // chunks
    f, r, h = lax.axis_index("frames"), lax.axis_index("rows"), lax.axis_index("heads")
    other = 1 - h
    partner = {"heads": other}

    def remote(src, dst, send, recv, to):
        return pltpu.make_async_remote_copy(
            src_ref=src, dst_ref=dst, send_sem=send, recv_sem=recv, device_id=to, device_id_type=MESH
        )

    def rows_of(c):
        return pl.ds(c * step, step)

    barrier = pltpu.get_barrier_semaphore()
    plane = [(a, b) for a in range(nr) for b in range(nh) if (a, b) != (0, 0)]

    def plane_to(a, b):
        return {"rows": lax.rem(r + a, nr), "heads": lax.rem(h + b, nh)}

    for a, b in plane:
        pl.semaphore_signal(barrier, inc=1, device_id=plane_to(a, b), device_id_type=MESH)
    for d in range(1, nf):
        pl.semaphore_signal(barrier, inc=1, device_id={"frames": lax.rem(f + d, nf)}, device_id_type=MESH)

    mine = r * nf + f
    loads = [
        pltpu.make_async_copy(src, dst, local_sem.at[i])
        for i, (src, dst) in enumerate(
            [
                (tokens, slots.at[h, mine]),
                (clip, x.at[1, h]),
                (w_time, wt),
                (w_out, wo.at[0]),
                (w_key, wk),
                (w_value, wv),
                (w_query, wq),
                (gain, gains),
            ]
        )
    ]
    for load in loads:
        load.start()

    tok[...] = jnp.zeros_like(tok)

    @pl.when(f == 0)
    def _():
        x[0] = jnp.zeros(x.shape[1:], BF16)

    @pl.when(f == nf - 1)
    def _():
        x[2] = jnp.zeros(x.shape[1:], BF16)

    pl.semaphore_wait(barrier, len(plane) + nf - 1)

    near = [
        remote(tokens, slots.at[h, mine], near_send.at[d], near_recv.at[d], {"frames": lax.rem(f + d, nf)})
        for d in range(1, nf)
    ]
    for copy in near:
        copy.start()

    def halo(side, c):
        to = f + 1 if side == 0 else f - 1
        slot = 0 if side == 0 else 2
        return remote(
            clip.at[rows_of(c)], x.at[slot, h, rows_of(c)], halo_send.at[side, c], halo_recv.at[side, c],
            {"frames": to},
        )

    def relay(side, c):
        slot = 0 if side == 0 else 2
        ref = x.at[slot, h, rows_of(c)]
        return remote(ref, ref, relay_send.at[side, c], relay_recv.at[side, c], partner)

    sends = (f < nf - 1, f > 0)
    gets = (f > 0, f < nf - 1)
    for c in range(chunks):
        for side in range(2):
            @pl.when(sends[side])
            def _():
                halo(side, c).start()

    pair = [
        remote(clip, x.at[1, h], pair_send.at[0], pair_recv.at[0], partner),
        remote(w_out, wo.at[1], pair_send.at[1], pair_recv.at[1], partner),
    ]
    for copy in pair:
        copy.start()

    def weight(o, which):
        return wt[o, pl.ds(pl.multiple_of(which * half, half), half), :]

    loads[1].wait()
    loads[2].wait()
    pair[0].wait_recv()
    first = jnp.concatenate([x[1, 0].astype(F32), x[1, 1].astype(F32)], axis=1)
    base[...] = first + dot(x[1, 0], wt[1, :half, :]) + dot(x[1, 1], wt[1, half:, :])

    loads[3].wait()
    pair[1].wait_recv()
    for k in range(2):
        whole = wo[k].astype(F32)
        wo_half[k] = jnp.where(h == 0, whole[:, :half], whole[:, half:]).astype(BF16)

    loads[0].wait()
    for copy in near:
        copy.wait_recv()
    line = slots.at[h, pl.ds(r * nf, nf)]
    far = [remote(line, line, far_send.at[a, b], far_recv.at[a, b], plane_to(a, b)) for a, b in plane]
    for copy in far:
        copy.start()

    def arrive(c):
        for side in range(2):
            @pl.when(gets[side])
            def _():
                halo(side, c).wait_recv()
                relay(side, c).start()
        rows = rows_of(c)
        base[rows] = base[rows] + dot(x[0, h, rows], weight(0, h)) + dot(x[2, h, rows], weight(2, h))

    def make_keys():
        for copy in far:
            copy.wait_recv()
        for k in range(nh):
            if nr * nf <= 16:
                for i in range(nr * nf):
                    tok[k, pl.ds(i * pad, count), :] = slots[k, i]
            else:
                def place(i, carry):
                    tok[k, pl.ds(pl.multiple_of(i * pad, pad), count), :] = slots[k, i]
                    return carry

                lax.fori_loop(0, nr * nf, place, 0)
        loads[4].wait()
        loads[5].wait()
        block = min(256, tok.shape[1])

        def project(i, carry):
            at = pl.ds(pl.multiple_of(i * block, block), block)
            head = lax.broadcasted_iota(jnp.int32, (block, half), 1)
            both = jnp.concatenate([tok[k, at, :] for k in range(nh)], axis=1)
            for weights, dest in ((wk, keys), (wv, values)):
                full = dot_t(both, weights[...])
                for k in range(local_heads):
                    inside = (head >= k * HEAD_SIZE) & (head < (k + 1) * HEAD_SIZE)
                    dest[k, at, :] = jnp.where(inside, full, 0.0).astype(BF16)
            return carry

        trips = tok.shape[1] // block
        if trips == 1:
            project(0, 0)
        else:
            lax.fori_loop(0, trips, project, 0)
        loads[6].wait()

    scale = 1.0 / (HEAD_SIZE ** 0.5)

    def attended(c):
        return remote(att.at[0, rows_of(c)], att.at[1, rows_of(c)], att_send.at[c], att_recv.at[c], partner)

    def process(c):
        rows = rows_of(c)
        for side in range(2):
            @pl.when(gets[side])
            def _():
                relay(side, c).wait_recv()
        summed = base[rows] + dot(x[0, other, rows], weight(0, other)) + dot(x[2, other, rows], weight(2, other))
        feats = summed.astype(BF16).astype(F32)
        base[rows] = feats
        centre = jnp.mean(feats, axis=-1, keepdims=True)
        moved = feats - centre
        spread = jnp.mean(moved * moved, axis=-1, keepdims=True)
        normed = (moved * lax.rsqrt(spread + 1e-05) * gain_row).astype(BF16)
        query = (dot_t(normed, wq[...]) * scale).astype(BF16)
        total_tokens = tok.shape[1]
        column = lax.broadcasted_iota(jnp.int32, (step, total_tokens), 1)
        valid = lax.rem(column, pad) < count

        def attend(k, result):
            scores = jnp.where(valid, dot_t(query, keys[k]), -3e38)
            expo = jnp.exp(scores - jnp.max(scores, axis=1, keepdims=True))
            total = jnp.sum(expo, axis=1, keepdims=True)
            return result + dot(expo.astype(BF16), values[k]) * (1.0 / total)

        result = jnp.zeros((step, half), F32)
        if total_tokens <= 1024:
            for k in range(local_heads):
                result = attend(k, result)
        else:
            result = lax.fori_loop(0, local_heads, attend, result)
        att[0, rows] = result.astype(BF16)
        attended(c).start()

    def finish(c):
        rows = rows_of(c)
        feats = base[rows]
        own = jnp.where(h == 0, feats[:, :half], feats[:, half:])
        mixed = own + dot(att[0, rows], wo_half[0])
        attended(c).wait_recv()
        out[rows] = (mixed + dot(att[1, rows], wo_half[1])).astype(BF16)

    loads[7].wait()
    gain_row = gains[...].reshape(1, -1)

    arrive(0)
    for c in range(1, min(2, chunks)):
        arrive(c)
    make_keys()
    for c in range(chunks):
        process(c)
        if c + 2 < chunks:
            arrive(c + 2)
        if c >= 1:
            finish(c - 1)
    finish(chunks - 1)

    for copy in near + pair + far:
        copy.wait_send()
    for c in range(chunks):
        attended(c).wait_send()
        for side in range(2):
            @pl.when(sends[side])
            def _():
                halo(side, c).wait_send()

            @pl.when(gets[side])
            def _():
                relay(side, c).wait_send()


def body(sizes, clip_latent, norm_gain, w_time, w_query, w_key, w_value, w_out, reference_tokens):
    nf, nr, nh = sizes
    shape = clip_latent.shape
    half, width = w_out.shape
    positions = shape[0] * shape[1] * shape[2]
    assert shape[0] == 1 and nh == 2
    chunks = next(n for n in (3, 2, 1) if positions % (16 * n) == 0)
    count = reference_tokens.shape[0]
    pad = -(-count // 16) * 16
    total = pad * nf * nr
    heads = half // HEAD_SIZE
    dma = pltpu.SemaphoreType.DMA
    result = pl.pallas_call(
        functools.partial(kernel, (nf, nr, nh, chunks, pad)),
        out_shape=jax.ShapeDtypeStruct((positions, half), BF16),
        in_specs=[pl.BlockSpec(memory_space=pl.ANY)] * 8,
        out_specs=pl.BlockSpec(memory_space=pltpu.VMEM),
        scratch_shapes=[
            pltpu.VMEM((3, 2, positions, half), BF16),
            pltpu.VMEM(w_time.shape, BF16),
            pltpu.VMEM((half, width), BF16),
            pltpu.VMEM((half, width), BF16),
            pltpu.VMEM((half, width), BF16),
            pltpu.VMEM((2, half, width), BF16),
            pltpu.VMEM((2, half, half), BF16),
            pltpu.VMEM((width,), F32),
            pltpu.VMEM((nh, nr * nf, count, half), BF16),
            pltpu.VMEM((nh, total, half), BF16),
            pltpu.VMEM((heads, total, half), BF16),
            pltpu.VMEM((heads, total, half), BF16),
            pltpu.VMEM((positions, width), F32),
            pltpu.VMEM((2, positions, half), BF16),
            dma((8,)),
            dma((2, chunks)),
            dma((2, chunks)),
            dma((2, chunks)),
            dma((2, chunks)),
            dma((2,)),
            dma((2,)),
            dma((nf,)),
            dma((nf,)),
            dma((nr, nh)),
            dma((nr, nh)),
            dma((chunks,)),
            dma((chunks,)),
        ],
        compiler_params=pltpu.CompilerParams(collective_id=0, has_side_effects=True),
    )(
        clip_latent.reshape(positions, half),
        norm_gain,
        w_time, w_query.T, w_key.T, w_value.T, w_out, reference_tokens,
    )
    return result.reshape(shape)


def solution(mesh):
    sizes = (mesh.shape["frames"], mesh.shape["rows"], mesh.shape["heads"])
    return jax.shard_map(
        functools.partial(body, sizes),
        mesh=mesh,
        in_specs=(
            P(("groups", "frames"), "rows", None, "heads"),
            P(),
            P(),
            P(None, "heads"),
            P(None, "heads"),
            P(None, "heads"),
            P("heads", None),
            P(("groups", "frames", "rows"), "heads"),
        ),
        out_specs=P(("groups", "frames"), "rows", None, "heads"),
        check_vma=False,
    )
```

```python
import functools

import jax
import jax.numpy as jnp
from jax import lax
from jax.experimental import pallas as pl
from jax.experimental.pallas import tpu as pltpu
from jax.sharding import PartitionSpec as P

HEAD_SIZE = 80
LANES = 128
BF16 = jnp.bfloat16
F32 = jnp.float32
MESH = pl.DeviceIdType.MESH


def dot_t(a, b):
    return lax.dot_general(a, b, (((1,), (1,)), ((), ())), preferred_element_type=F32)


def dot(a, b):
    return jnp.dot(a, b, preferred_element_type=F32)


def kernel(
    sizes,
    clip, gain, w_time, w_query, w_key, w_value, w_out, tokens,
    out,
    x, wt, wq, wkv, wo, wo_half, gains, slots, tok, keys, values, base, att,
    local_sem, halo_send, halo_recv, relay_send, relay_recv, pair_send, pair_recv,
    near_send, near_recv, far_send, far_recv, att_send, att_recv,
):
    nf, nr, nh, chunks, pad = sizes
    positions, half = clip.shape
    count = tokens.shape[0]
    local_heads = half // HEAD_SIZE
    step = positions // chunks
    f, r, h = lax.axis_index("frames"), lax.axis_index("rows"), lax.axis_index("heads")
    other = 1 - h
    partner = {"heads": other}

    def remote(src, dst, send, recv, to):
        return pltpu.make_async_remote_copy(
            src_ref=src, dst_ref=dst, send_sem=send, recv_sem=recv, device_id=to, device_id_type=MESH
        )

    def rows_of(c):
        return pl.ds(c * step, step)

    barrier = pltpu.get_barrier_semaphore()
    plane = [(a, b) for a in range(nr) for b in range(nh) if (a, b) != (0, 0)]

    def plane_to(a, b):
        return {"rows": lax.rem(r + a, nr), "heads": lax.rem(h + b, nh)}

    for a, b in plane:
        pl.semaphore_signal(barrier, inc=1, device_id=plane_to(a, b), device_id_type=MESH)
    for d in range(1, nf):
        pl.semaphore_signal(barrier, inc=1, device_id={"frames": lax.rem(f + d, nf)}, device_id_type=MESH)

    mine = r * nf + f
    loads = [
        pltpu.make_async_copy(src, dst, local_sem.at[i])
        for i, (src, dst) in enumerate(
            [
                (tokens, slots.at[h, mine]),
                (clip, x.at[1, h]),
                (w_time, wt),
                (w_out, wo.at[0]),
                (gain, gains),
            ]
            + [
                (weights.at[pl.ds(k * HEAD_SIZE, HEAD_SIZE)], dest.at[pl.ds((first + k) * LANES, HEAD_SIZE)])
                for weights, dest, first in ((w_key, wkv, 0), (w_value, wkv, local_heads), (w_query, wq, 0))
                for k in range(local_heads)
            ]
        )
    ]
    rest = LANES - HEAD_SIZE
    for dest in (wq, wkv):
        for k in range(dest.shape[0] // LANES):
            dest[pl.ds(k * LANES + HEAD_SIZE, rest), :] = jnp.zeros((rest, dest.shape[1]), BF16)
    for load in loads:
        load.start()

    tok[...] = jnp.zeros_like(tok)
    values[:, :, LANES:] = jnp.ones((local_heads, tok.shape[1], LANES), BF16)
    for k in range(2):
        for i in range(local_heads):
            wo_half[k, pl.ds(i * LANES + HEAD_SIZE, rest), :] = jnp.zeros((rest, half), BF16)

    @pl.when(f == 0)
    def _():
        x[0] = jnp.zeros(x.shape[1:], BF16)

    @pl.when(f == nf - 1)
    def _():
        x[2] = jnp.zeros(x.shape[1:], BF16)

    pl.semaphore_wait(barrier, len(plane) + nf - 1)

    near = [
        remote(tokens, slots.at[h, mine], near_send.at[d], near_recv.at[d], {"frames": lax.rem(f + d, nf)})
        for d in range(1, nf)
    ]
    for copy in near:
        copy.start()

    def halo(side, c):
        to = f + 1 if side == 0 else f - 1
        slot = 0 if side == 0 else 2
        return remote(
            clip.at[rows_of(c)], x.at[slot, h, rows_of(c)], halo_send.at[side, c], halo_recv.at[side, c],
            {"frames": to},
        )

    def relay(side, c):
        slot = 0 if side == 0 else 2
        ref = x.at[slot, h, rows_of(c)]
        return remote(ref, ref, relay_send.at[side, c], relay_recv.at[side, c], partner)

    sends = (f < nf - 1, f > 0)
    gets = (f > 0, f < nf - 1)
    for c in range(chunks):
        for side in range(2):
            @pl.when(sends[side])
            def _():
                halo(side, c).start()

    pair = [
        remote(clip, x.at[1, h], pair_send.at[0], pair_recv.at[0], partner),
        remote(w_out, wo.at[1], pair_send.at[1], pair_recv.at[1], partner),
    ]
    pair[0].start()

    def weight(o, which):
        return wt[o, pl.ds(pl.multiple_of(which * half, half), half), :]

    def sides(which, rows):
        both = jnp.concatenate([x[0, which, rows], x[2, which, rows]], axis=1)
        return dot(both, jnp.concatenate([weight(0, which), weight(2, which)], axis=0))

    loads[1].wait()
    loads[2].wait()
    pair[0].wait_recv()
    centre_full = jnp.concatenate([x[1, 0], x[1, 1]], axis=1)
    base[...] = centre_full.astype(F32) + dot(centre_full, wt[1])

    loads[0].wait()
    for copy in near:
        copy.wait_recv()
    line = slots.at[h, pl.ds(r * nf, nf)]
    far = [remote(line, line, far_send.at[a, b], far_recv.at[a, b], plane_to(a, b)) for a, b in plane]
    for copy in far:
        copy.start()
    pair[1].start()

    def prepare():
        loads[3].wait()
        pair[1].wait_recv()
        for k in range(2):
            whole = wo[k].astype(F32)
            part = jnp.where(h == 0, whole[:, :half], whole[:, half:]).astype(BF16)
            for i in range(local_heads):
                wo_half[k, pl.ds(i * LANES, HEAD_SIZE), :] = part[i * HEAD_SIZE : (i + 1) * HEAD_SIZE, :]

    def arrive(c):
        for side in range(2):
            @pl.when(gets[side])
            def _():
                halo(side, c).wait_recv()
                relay(side, c).start()
        rows = rows_of(c)
        base[rows] = base[rows] + sides(h, rows)

    def make_keys():
        for copy in far:
            copy.wait_recv()
        for k in range(nh):
            if nr * nf <= 16:
                for i in range(nr * nf):
                    tok[k, pl.ds(i * pad, count), :] = slots[k, i]
            else:
                def place(i, carry):
                    tok[k, pl.ds(pl.multiple_of(i * pad, pad), count), :] = slots[k, i]
                    return carry

                lax.fori_loop(0, nr * nf, place, 0)
        for load in loads[5:]:
            load.wait()
        block = min(256, tok.shape[1])

        def project(i, carry):
            at = pl.ds(pl.multiple_of(i * block, block), block)
            both = jnp.concatenate([tok[k, at, :] for k in range(nh)], axis=1)
            full = dot_t(both, wkv[...]).astype(BF16)
            for k in range(local_heads):
                keys[k, at, :] = full[:, k * LANES : (k + 1) * LANES]
                values[k, at, :LANES] = full[:, (local_heads + k) * LANES : (local_heads + k + 1) * LANES]
            return carry

        trips = tok.shape[1] // block
        if trips == 1:
            project(0, 0)
        else:
            lax.fori_loop(0, trips, project, 0)

    scale = 1.0 / (HEAD_SIZE ** 0.5)

    def attended(c, k):
        rows = rows_of(c)
        return remote(att.at[0, k, rows], att.at[1, k, rows], att_send.at[c, k], att_recv.at[c, k], partner)

    def process(c):
        rows = rows_of(c)
        for side in range(2):
            @pl.when(gets[side])
            def _():
                relay(side, c).wait_recv()
        summed = base[rows] + sides(other, rows)
        feats = summed.astype(BF16).astype(F32)
        base[rows] = feats
        centre = jnp.mean(feats, axis=-1, keepdims=True)
        moved = feats - centre
        spread = jnp.mean(moved * moved, axis=-1, keepdims=True)
        normed = (moved * lax.rsqrt(spread + 1e-05) * gain_row).astype(BF16)
        query = (dot_t(normed, wq[...]) * scale).astype(BF16)
        total_tokens = tok.shape[1]
        column = lax.broadcasted_iota(jnp.int32, (step, total_tokens), 1)
        valid = lax.rem(column, pad) < count

        for k in range(local_heads):
            scores = jnp.where(valid, dot_t(query[:, k * LANES : (k + 1) * LANES], keys[k]), -3e38)
            probs = jnp.exp(scores - jnp.max(scores, axis=1, keepdims=True)).astype(BF16)
            mixed = dot(probs, values[k])
            att[0, k, rows] = (mixed[:, :LANES] / mixed[:, LANES:]).astype(BF16)
            attended(c, k).start()

    def finish(c):
        rows = rows_of(c)
        feats = base[rows]
        own = jnp.where(h == 0, feats[:, :half], feats[:, half:])

        def joined(which):
            return jnp.concatenate([att[which, k, rows] for k in range(local_heads)], axis=1)

        mixed = own + dot(joined(0), wo_half[0])
        for k in range(local_heads):
            attended(c, k).wait_recv()
        out[rows] = (mixed + dot(joined(1), wo_half[1])).astype(BF16)

    loads[4].wait()
    gain_row = gains[...].reshape(1, -1)

    make_keys()
    arrive(0)
    for c in range(1, min(2, chunks)):
        arrive(c)
    prepare()
    for c in range(chunks):
        process(c)
        if c + 2 < chunks:
            arrive(c + 2)
        if c >= 1:
            finish(c - 1)
    finish(chunks - 1)

    for copy in near + pair + far:
        copy.wait_send()
    for c in range(chunks):
        for k in range(local_heads):
            attended(c, k).wait_send()
        for side in range(2):
            @pl.when(sends[side])
            def _():
                halo(side, c).wait_send()

            @pl.when(gets[side])
            def _():
                relay(side, c).wait_send()


def body(sizes, clip_latent, norm_gain, w_time, w_query, w_key, w_value, w_out, reference_tokens):
    nf, nr, nh = sizes
    shape = clip_latent.shape
    half, width = w_out.shape
    positions = shape[0] * shape[1] * shape[2]
    assert shape[0] == 1 and nh == 2
    chunks = next(n for n in (1,) if positions % (16 * n) == 0)
    count = reference_tokens.shape[0]
    pad = -(-count // 16) * 16
    total = pad * nf * nr
    heads = half // HEAD_SIZE
    dma = pltpu.SemaphoreType.DMA
    result = pl.pallas_call(
        functools.partial(kernel, (nf, nr, nh, chunks, pad)),
        out_shape=jax.ShapeDtypeStruct((positions, half), BF16),
        in_specs=[pl.BlockSpec(memory_space=pl.ANY)] * 8,
        out_specs=pl.BlockSpec(memory_space=pltpu.VMEM),
        scratch_shapes=[
            pltpu.VMEM((3, 2, positions, half), BF16),
            pltpu.VMEM(w_time.shape, BF16),
            pltpu.VMEM((heads * LANES, width), BF16),
            pltpu.VMEM((2 * heads * LANES, width), BF16),
            pltpu.VMEM((2, half, width), BF16),
            pltpu.VMEM((2, heads * LANES, half), BF16),
            pltpu.VMEM((width,), F32),
            pltpu.VMEM((nh, nr * nf, count, half), BF16),
            pltpu.VMEM((nh, total, half), BF16),
            pltpu.VMEM((heads, total, LANES), BF16),
            pltpu.VMEM((heads, total, 2 * LANES), BF16),
            pltpu.VMEM((positions, width), F32),
            pltpu.VMEM((2, heads, positions, LANES), BF16),
            dma((5 + 3 * heads,)),
            dma((2, chunks)),
            dma((2, chunks)),
            dma((2, chunks)),
            dma((2, chunks)),
            dma((2,)),
            dma((2,)),
            dma((nf,)),
            dma((nf,)),
            dma((nr, nh)),
            dma((nr, nh)),
            dma((chunks, heads)),
            dma((chunks, heads)),
        ],
        compiler_params=pltpu.CompilerParams(collective_id=0, has_side_effects=True),
    )(
        clip_latent.reshape(positions, half),
        norm_gain,
        w_time, w_query.T, w_key.T, w_value.T, w_out, reference_tokens,
    )
    return result.reshape(shape)


def solution(mesh):
    sizes = (mesh.shape["frames"], mesh.shape["rows"], mesh.shape["heads"])
    return jax.shard_map(
        functools.partial(body, sizes),
        mesh=mesh,
        in_specs=(
            P(("groups", "frames"), "rows", None, "heads"),
            P(),
            P(),
            P(None, "heads"),
            P(None, "heads"),
            P(None, "heads"),
            P("heads", None),
            P(("groups", "frames", "rows"), "heads"),
        ),
        out_specs=P(("groups", "frames"), "rows", None, "heads"),
        check_vma=False,
    )
```

```python
import functools

import jax
import jax.numpy as jnp
from jax import lax
from jax.experimental import pallas as pl
from jax.experimental.pallas import tpu as pltpu
from jax.sharding import PartitionSpec as P

HEAD_SIZE = 80
LANES = 128
BF16 = jnp.bfloat16
F32 = jnp.float32
MESH = pl.DeviceIdType.MESH


def dot_t(a, b):
    return lax.dot_general(a, b, (((1,), (1,)), ((), ())), preferred_element_type=F32)


def dot(a, b):
    return jnp.dot(a, b, preferred_element_type=F32)


def kernel(
    sizes,
    clip, gain, w_time, w_query, w_key, w_value, w_out, tokens,
    out,
    x, wt, wq, wkv, wo, gains, slots, tok, keys, values, base, att,
    local_sem, halo_send, halo_recv, relay_send, relay_recv, pair_send, pair_recv,
    near_send, near_recv, far_send, far_recv, att_send, att_recv,
):
    nf, nr, nh, chunks, pad = sizes
    positions, half = clip.shape
    count = tokens.shape[0]
    local_heads = half // HEAD_SIZE
    step = positions // chunks
    f, r, h = lax.axis_index("frames"), lax.axis_index("rows"), lax.axis_index("heads")
    other = 1 - h
    partner = {"heads": other}

    def remote(src, dst, send, recv, to):
        return pltpu.make_async_remote_copy(
            src_ref=src, dst_ref=dst, send_sem=send, recv_sem=recv, device_id=to, device_id_type=MESH
        )

    def rows_of(c):
        return pl.ds(c * step, step)

    barrier = pltpu.get_barrier_semaphore()
    plane = [(a, b) for a in range(nr) for b in range(nh) if (a, b) != (0, 0)]

    def plane_to(a, b):
        return {"rows": lax.rem(r + a, nr), "heads": lax.rem(h + b, nh)}

    for a, b in plane:
        pl.semaphore_signal(barrier, inc=1, device_id=plane_to(a, b), device_id_type=MESH)
    for d in range(1, nf):
        pl.semaphore_signal(barrier, inc=1, device_id={"frames": lax.rem(f + d, nf)}, device_id_type=MESH)

    mine = r * nf + f
    loads = [
        pltpu.make_async_copy(src, dst, local_sem.at[i])
        for i, (src, dst) in enumerate(
            [
                (tokens, slots.at[h, mine]),
                (clip, x.at[1, h]),
                (w_time, wt),
                (gain, gains),
            ]
            + [
                (weights.at[pl.ds(k * HEAD_SIZE, HEAD_SIZE)], dest.at[pl.ds((first + k) * LANES, HEAD_SIZE)])
                for weights, dest, first in ((w_key, wkv, 0), (w_value, wkv, local_heads), (w_query, wq, 0), (w_out, wo, 0))
                for k in range(local_heads)
            ]
        )
    ]
    rest = LANES - HEAD_SIZE
    for dest in (wq, wkv, wo):
        for k in range(dest.shape[0] // LANES):
            dest[pl.ds(k * LANES + HEAD_SIZE, rest), :] = jnp.zeros((rest, dest.shape[1]), BF16)
    for load in loads:
        load.start()

    tok[...] = jnp.zeros_like(tok)
    values[:, :, LANES:] = jnp.ones((local_heads, tok.shape[1], LANES), BF16)

    @pl.when(f == 0)
    def _():
        x[0] = jnp.zeros(x.shape[1:], BF16)

    @pl.when(f == nf - 1)
    def _():
        x[2] = jnp.zeros(x.shape[1:], BF16)

    pl.semaphore_wait(barrier, len(plane) + nf - 1)

    near = [
        remote(tokens, slots.at[h, mine], near_send.at[d], near_recv.at[d], {"frames": lax.rem(f + d, nf)})
        for d in range(1, nf)
    ]
    for copy in near:
        copy.start()

    def halo(side, c):
        to = f + 1 if side == 0 else f - 1
        slot = 0 if side == 0 else 2
        return remote(
            clip.at[rows_of(c)], x.at[slot, h, rows_of(c)], halo_send.at[side, c], halo_recv.at[side, c],
            {"frames": to},
        )

    def relay(side, c):
        slot = 0 if side == 0 else 2
        ref = x.at[slot, h, rows_of(c)]
        return remote(ref, ref, relay_send.at[side, c], relay_recv.at[side, c], partner)

    sends = (f < nf - 1, f > 0)
    gets = (f > 0, f < nf - 1)
    for c in range(chunks):
        for side in range(2):
            @pl.when(sends[side])
            def _():
                halo(side, c).start()

    pair = [remote(clip, x.at[1, h], pair_send.at[0], pair_recv.at[0], partner)]
    pair[0].start()

    def weight(o, which):
        return wt[o, pl.ds(pl.multiple_of(which * half, half), half), :]

    def sides(which, rows):
        both = jnp.concatenate([x[0, which, rows], x[2, which, rows]], axis=1)
        return dot(both, jnp.concatenate([weight(0, which), weight(2, which)], axis=0))

    loads[1].wait()
    loads[2].wait()
    pair[0].wait_recv()
    centre_full = jnp.concatenate([x[1, 0], x[1, 1]], axis=1)
    base[...] = centre_full.astype(F32) + dot(centre_full, wt[1])

    loads[0].wait()
    for copy in near:
        copy.wait_recv()
    line = slots.at[h, pl.ds(r * nf, nf)]
    far = [remote(line, line, far_send.at[a, b], far_recv.at[a, b], plane_to(a, b)) for a, b in plane]
    for copy in far:
        copy.start()

    def arrive(c):
        for side in range(2):
            @pl.when(gets[side])
            def _():
                halo(side, c).wait_recv()
                relay(side, c).start()
        rows = rows_of(c)
        base[rows] = base[rows] + sides(h, rows)

    def make_keys():
        for copy in far:
            copy.wait_recv()
        for k in range(nh):
            if nr * nf <= 16:
                for i in range(nr * nf):
                    tok[k, pl.ds(i * pad, count), :] = slots[k, i]
            else:
                def place(i, carry):
                    tok[k, pl.ds(pl.multiple_of(i * pad, pad), count), :] = slots[k, i]
                    return carry

                lax.fori_loop(0, nr * nf, place, 0)
        for load in loads[4:]:
            load.wait()
        block = min(256, tok.shape[1])

        def project(i, carry):
            at = pl.ds(pl.multiple_of(i * block, block), block)
            both = jnp.concatenate([tok[k, at, :] for k in range(nh)], axis=1)
            full = dot_t(both, wkv[...]).astype(BF16)
            for k in range(local_heads):
                keys[k, at, :] = full[:, k * LANES : (k + 1) * LANES]
                values[k, at, :LANES] = full[:, (local_heads + k) * LANES : (local_heads + k + 1) * LANES]
            return carry

        trips = tok.shape[1] // block
        if trips == 1:
            project(0, 0)
        else:
            lax.fori_loop(0, trips, project, 0)

    scale = 1.0 / (HEAD_SIZE ** 0.5)

    def share(c):
        rows = rows_of(c)
        return remote(att.at[0, rows], att.at[1, rows], att_send.at[c], att_recv.at[c], partner)

    def process(c):
        rows = rows_of(c)
        for side in range(2):
            @pl.when(gets[side])
            def _():
                relay(side, c).wait_recv()
        summed = base[rows] + sides(other, rows)
        feats = summed.astype(BF16).astype(F32)
        base[rows] = feats
        centre = jnp.mean(feats, axis=-1, keepdims=True)
        moved = feats - centre
        spread = jnp.mean(moved * moved, axis=-1, keepdims=True)
        normed = (moved * lax.rsqrt(spread + 1e-05) * gain_row).astype(BF16)
        query = (dot_t(normed, wq[...]) * scale).astype(BF16)
        total_tokens = tok.shape[1]
        column = lax.broadcasted_iota(jnp.int32, (step, total_tokens), 1)
        valid = lax.rem(column, pad) < count

        attended = []
        for k in range(local_heads):
            scores = jnp.where(valid, dot_t(query[:, k * LANES : (k + 1) * LANES], keys[k]), -3e38)
            probs = jnp.exp(scores - jnp.max(scores, axis=1, keepdims=True)).astype(BF16)
            mixed = dot(probs, values[k])
            attended.append((mixed[:, :LANES] / mixed[:, LANES:]).astype(BF16))
        mixed = dot(jnp.concatenate(attended, axis=1), wo[...])
        low, high = mixed[:, :half], mixed[:, half:]
        att[0, rows] = jnp.where(h == 0, high, low).astype(BF16)
        share(c).start()
        total = base[rows] + mixed
        base[rows, :half] = jnp.where(h == 0, total[:, :half], total[:, half:])

    def finish(c):
        rows = rows_of(c)
        share(c).wait_recv()
        out[rows] = (base[rows, :half] + att[1, rows].astype(F32)).astype(BF16)

    loads[3].wait()
    gain_row = gains[...].reshape(1, -1)

    make_keys()
    arrive(0)
    for c in range(1, min(2, chunks)):
        arrive(c)
    for c in range(chunks):
        process(c)
        if c + 2 < chunks:
            arrive(c + 2)
        if c >= 1:
            finish(c - 1)
    finish(chunks - 1)

    for copy in near + pair + far:
        copy.wait_send()
    for c in range(chunks):
        share(c).wait_send()
        for side in range(2):
            @pl.when(sends[side])
            def _():
                halo(side, c).wait_send()

            @pl.when(gets[side])
            def _():
                relay(side, c).wait_send()


def body(sizes, clip_latent, norm_gain, w_time, w_query, w_key, w_value, w_out, reference_tokens):
    nf, nr, nh = sizes
    shape = clip_latent.shape
    half, width = w_out.shape
    positions = shape[0] * shape[1] * shape[2]
    assert shape[0] == 1 and nh == 2
    chunks = next(n for n in (1,) if positions % (16 * n) == 0)
    count = reference_tokens.shape[0]
    pad = -(-count // 16) * 16
    total = pad * nf * nr
    heads = half // HEAD_SIZE
    dma = pltpu.SemaphoreType.DMA
    result = pl.pallas_call(
        functools.partial(kernel, (nf, nr, nh, chunks, pad)),
        out_shape=jax.ShapeDtypeStruct((positions, half), BF16),
        in_specs=[pl.BlockSpec(memory_space=pl.ANY)] * 8,
        out_specs=pl.BlockSpec(memory_space=pltpu.VMEM),
        scratch_shapes=[
            pltpu.VMEM((3, 2, positions, half), BF16),
            pltpu.VMEM(w_time.shape, BF16),
            pltpu.VMEM((heads * LANES, width), BF16),
            pltpu.VMEM((2 * heads * LANES, width), BF16),
            pltpu.VMEM((heads * LANES, width), BF16),
            pltpu.VMEM((width,), F32),
            pltpu.VMEM((nh, nr * nf, count, half), BF16),
            pltpu.VMEM((nh, total, half), BF16),
            pltpu.VMEM((heads, total, LANES), BF16),
            pltpu.VMEM((heads, total, 2 * LANES), BF16),
            pltpu.VMEM((positions, width), F32),
            pltpu.VMEM((2, positions, half), BF16),
            dma((4 + 4 * heads,)),
            dma((2, chunks)),
            dma((2, chunks)),
            dma((2, chunks)),
            dma((2, chunks)),
            dma((1,)),
            dma((1,)),
            dma((nf,)),
            dma((nf,)),
            dma((nr, nh)),
            dma((nr, nh)),
            dma((chunks,)),
            dma((chunks,)),
        ],
        compiler_params=pltpu.CompilerParams(collective_id=0, has_side_effects=True),
    )(
        clip_latent.reshape(positions, half),
        norm_gain,
        w_time, w_query.T, w_key.T, w_value.T, w_out, reference_tokens,
    )
    return result.reshape(shape)


def solution(mesh):
    sizes = (mesh.shape["frames"], mesh.shape["rows"], mesh.shape["heads"])
    return jax.shard_map(
        functools.partial(body, sizes),
        mesh=mesh,
        in_specs=(
            P(("groups", "frames"), "rows", None, "heads"),
            P(),
            P(),
            P(None, "heads"),
            P(None, "heads"),
            P(None, "heads"),
            P("heads", None),
            P(("groups", "frames", "rows"), "heads"),
        ),
        out_specs=P(("groups", "frames"), "rows", None, "heads"),
        check_vma=False,
    )
```

```python
import functools

import jax
import jax.numpy as jnp
from jax import lax
from jax.experimental import pallas as pl
from jax.experimental.pallas import tpu as pltpu
from jax.sharding import PartitionSpec as P

HEAD_SIZE = 80
LANES = 128
BF16 = jnp.bfloat16
F32 = jnp.float32
MESH = pl.DeviceIdType.MESH


def dot_t(a, b):
    return lax.dot_general(a, b, (((1,), (1,)), ((), ())), preferred_element_type=F32)


def dot(a, b):
    return jnp.dot(a, b, preferred_element_type=F32)


def kernel(
    sizes,
    clip, gain, w_time, w_query, w_key, w_value, w_out, tokens,
    out,
    x, wt, wq, wkv, wqt, wkvt, wo, gains, slots, tok, keys, values, base, att,
    local_sem, halo_send, halo_recv, relay_send, relay_recv, pair_send, pair_recv,
    near_send, near_recv, far_send, far_recv, att_send, att_recv,
):
    nf, nr, nh, chunks, pad = sizes
    positions, half = clip.shape
    count = tokens.shape[0]
    local_heads = half // HEAD_SIZE
    step = positions // chunks
    f, r, h = lax.axis_index("frames"), lax.axis_index("rows"), lax.axis_index("heads")
    other = 1 - h
    partner = {"heads": other}

    def remote(src, dst, send, recv, to):
        return pltpu.make_async_remote_copy(
            src_ref=src, dst_ref=dst, send_sem=send, recv_sem=recv, device_id=to, device_id_type=MESH
        )

    def rows_of(c):
        return pl.ds(c * step, step)

    barrier = pltpu.get_barrier_semaphore()
    plane = [(a, b) for a in range(nr) for b in range(nh) if (a, b) != (0, 0)]

    def plane_to(a, b):
        return {"rows": lax.rem(r + a, nr), "heads": lax.rem(h + b, nh)}

    for a, b in plane:
        pl.semaphore_signal(barrier, inc=1, device_id=plane_to(a, b), device_id_type=MESH)
    for d in range(1, nf):
        pl.semaphore_signal(barrier, inc=1, device_id={"frames": lax.rem(f + d, nf)}, device_id_type=MESH)

    mine = r * nf + f
    loads = [
        pltpu.make_async_copy(src, dst, local_sem.at[i])
        for i, (src, dst) in enumerate(
            [
                (tokens, slots.at[h, mine]),
                (clip, x.at[1, h]),
                (w_time, wt),
                (gain, gains),
            ]
            + [
                (weights.at[pl.ds(k * HEAD_SIZE, HEAD_SIZE)], dest.at[pl.ds((first + k) * LANES, HEAD_SIZE)])
                for weights, dest, first in ((w_key, wkv, 0), (w_value, wkv, local_heads), (w_query, wq, 0), (w_out, wo, 0))
                for k in range(local_heads)
            ]
        )
    ]
    rest = LANES - HEAD_SIZE
    for dest in (wq, wkv, wo):
        for k in range(dest.shape[0] // LANES):
            dest[pl.ds(k * LANES + HEAD_SIZE, rest), :] = jnp.zeros((rest, dest.shape[1]), BF16)
    for load in loads[:2] + loads[3:] + loads[2:3]:
        load.start()

    tok[...] = jnp.zeros_like(tok)
    values[:, :, LANES:] = jnp.ones((local_heads, tok.shape[1], LANES), BF16)

    @pl.when(f == 0)
    def _():
        x[0] = jnp.zeros(x.shape[1:], BF16)

    @pl.when(f == nf - 1)
    def _():
        x[2] = jnp.zeros(x.shape[1:], BF16)

    pl.semaphore_wait(barrier, len(plane) + nf - 1)

    near = [
        remote(tokens, slots.at[h, mine], near_send.at[d], near_recv.at[d], {"frames": lax.rem(f + d, nf)})
        for d in range(1, nf)
    ]
    for copy in near:
        copy.start()

    def halo(side, c):
        to = f + 1 if side == 0 else f - 1
        slot = 0 if side == 0 else 2
        return remote(
            clip.at[rows_of(c)], x.at[slot, h, rows_of(c)], halo_send.at[side, c], halo_recv.at[side, c],
            {"frames": to},
        )

    def relay(side, c):
        slot = 0 if side == 0 else 2
        ref = x.at[slot, h, rows_of(c)]
        return remote(ref, ref, relay_send.at[side, c], relay_recv.at[side, c], partner)

    sends = (f < nf - 1, f > 0)
    gets = (f > 0, f < nf - 1)
    for c in range(chunks):
        for side in range(2):
            @pl.when(sends[side])
            def _():
                halo(side, c).start()

    pair = [remote(clip, x.at[1, h], pair_send.at[0], pair_recv.at[0], partner)]
    pair[0].start()

    def weight(o, which):
        return wt[o, pl.ds(pl.multiple_of(which * half, half), half), :]

    def sides(which, rows):
        both = jnp.concatenate([x[0, which, rows], x[2, which, rows]], axis=1)
        return dot(both, jnp.concatenate([weight(0, which), weight(2, which)], axis=0))

    for load in loads[4:]:
        load.wait()
    wkvt[...] = wkv[...].T
    wqt[...] = wq[...].T
    loads[0].wait()
    for copy in near:
        copy.wait_recv()
    line = slots.at[h, pl.ds(r * nf, nf)]
    far = [remote(line, line, far_send.at[a, b], far_recv.at[a, b], plane_to(a, b)) for a, b in plane]
    for copy in far:
        copy.start()

    loads[1].wait()
    loads[2].wait()
    pair[0].wait_recv()
    centre_full = jnp.concatenate([x[1, 0], x[1, 1]], axis=1)
    base[...] = centre_full.astype(F32) + dot(centre_full, wt[1])

    def arrive(c):
        for side in range(2):
            @pl.when(gets[side])
            def _():
                halo(side, c).wait_recv()
                relay(side, c).start()
        rows = rows_of(c)
        base[rows] = base[rows] + sides(h, rows)

    def make_keys():
        for copy in far:
            copy.wait_recv()
        for k in range(nh):
            if nr * nf <= 16:
                for i in range(nr * nf):
                    tok[k, pl.ds(i * pad, count), :] = slots[k, i]
            else:
                def place(i, carry):
                    tok[k, pl.ds(pl.multiple_of(i * pad, pad), count), :] = slots[k, i]
                    return carry

                lax.fori_loop(0, nr * nf, place, 0)
        block = min(256, tok.shape[1])

        def project(i, carry):
            at = pl.ds(pl.multiple_of(i * block, block), block)
            both = jnp.concatenate([tok[k, at, :] for k in range(nh)], axis=1)
            full = dot(both, wkvt[...]).astype(BF16)
            for k in range(local_heads):
                keys[k, at, :] = full[:, k * LANES : (k + 1) * LANES]
                values[k, at, :LANES] = full[:, (local_heads + k) * LANES : (local_heads + k + 1) * LANES]
            return carry

        trips = tok.shape[1] // block
        if trips == 1:
            project(0, 0)
        else:
            lax.fori_loop(0, trips, project, 0)

    scale = 1.0 / (HEAD_SIZE ** 0.5)

    def share(c):
        rows = rows_of(c)
        return remote(att.at[0, rows], att.at[1, rows], att_send.at[c], att_recv.at[c], partner)

    def process(c):
        rows = rows_of(c)
        for side in range(2):
            @pl.when(gets[side])
            def _():
                relay(side, c).wait_recv()
        summed = base[rows] + sides(other, rows)
        feats = summed.astype(BF16).astype(F32)
        base[rows] = feats
        centre = jnp.mean(feats, axis=-1, keepdims=True)
        moved = feats - centre
        spread = jnp.mean(moved * moved, axis=-1, keepdims=True)
        normed = (moved * lax.rsqrt(spread + 1e-05) * gain_row).astype(BF16)
        query = (dot(normed, wqt[...]) * scale).astype(BF16)
        total_tokens = tok.shape[1]
        column = lax.broadcasted_iota(jnp.int32, (step, total_tokens), 1)
        valid = lax.rem(column, pad) < count

        attended = []
        for k in range(local_heads):
            scores = jnp.where(valid, dot_t(query[:, k * LANES : (k + 1) * LANES], keys[k]), -3e38)
            probs = jnp.exp(scores - jnp.max(scores, axis=1, keepdims=True)).astype(BF16)
            mixed = dot(probs, values[k])
            attended.append((mixed[:, :LANES] / mixed[:, LANES:]).astype(BF16))
        mixed = dot(jnp.concatenate(attended, axis=1), wo[...])
        low, high = mixed[:, :half], mixed[:, half:]
        att[0, rows] = jnp.where(h == 0, high, low).astype(BF16)
        share(c).start()
        total = base[rows] + mixed
        base[rows, :half] = jnp.where(h == 0, total[:, :half], total[:, half:])

    def finish(c):
        rows = rows_of(c)
        share(c).wait_recv()
        out[rows] = (base[rows, :half] + att[1, rows].astype(F32)).astype(BF16)

    loads[3].wait()
    gain_row = gains[...].reshape(1, -1)

    make_keys()
    arrive(0)
    for c in range(1, min(2, chunks)):
        arrive(c)
    for c in range(chunks):
        process(c)
        if c + 2 < chunks:
            arrive(c + 2)
        if c >= 1:
            finish(c - 1)
    finish(chunks - 1)

    for copy in near + pair + far:
        copy.wait_send()
    for c in range(chunks):
        share(c).wait_send()
        for side in range(2):
            @pl.when(sends[side])
            def _():
                halo(side, c).wait_send()

            @pl.when(gets[side])
            def _():
                relay(side, c).wait_send()


def body(sizes, clip_latent, norm_gain, w_time, w_query, w_key, w_value, w_out, reference_tokens):
    nf, nr, nh = sizes
    shape = clip_latent.shape
    half, width = w_out.shape
    positions = shape[0] * shape[1] * shape[2]
    assert shape[0] == 1 and nh == 2
    chunks = next(n for n in (1,) if positions % (16 * n) == 0)
    count = reference_tokens.shape[0]
    pad = -(-count // 16) * 16
    total = pad * nf * nr
    heads = half // HEAD_SIZE
    dma = pltpu.SemaphoreType.DMA
    result = pl.pallas_call(
        functools.partial(kernel, (nf, nr, nh, chunks, pad)),
        out_shape=jax.ShapeDtypeStruct((positions, half), BF16),
        in_specs=[pl.BlockSpec(memory_space=pl.ANY)] * 8,
        out_specs=pl.BlockSpec(memory_space=pltpu.VMEM),
        scratch_shapes=[
            pltpu.VMEM((3, 2, positions, half), BF16),
            pltpu.VMEM(w_time.shape, BF16),
            pltpu.VMEM((heads * LANES, width), BF16),
            pltpu.VMEM((2 * heads * LANES, width), BF16),
            pltpu.VMEM((width, heads * LANES), BF16),
            pltpu.VMEM((width, 2 * heads * LANES), BF16),
            pltpu.VMEM((heads * LANES, width), BF16),
            pltpu.VMEM((width,), F32),
            pltpu.VMEM((nh, nr * nf, count, half), BF16),
            pltpu.VMEM((nh, total, half), BF16),
            pltpu.VMEM((heads, total, LANES), BF16),
            pltpu.VMEM((heads, total, 2 * LANES), BF16),
            pltpu.VMEM((positions, width), F32),
            pltpu.VMEM((2, positions, half), BF16),
            dma((4 + 4 * heads,)),
            dma((2, chunks)),
            dma((2, chunks)),
            dma((2, chunks)),
            dma((2, chunks)),
            dma((1,)),
            dma((1,)),
            dma((nf,)),
            dma((nf,)),
            dma((nr, nh)),
            dma((nr, nh)),
            dma((chunks,)),
            dma((chunks,)),
        ],
        compiler_params=pltpu.CompilerParams(collective_id=0, has_side_effects=True),
    )(
        clip_latent.reshape(positions, half),
        norm_gain,
        w_time, w_query.T, w_key.T, w_value.T, w_out, reference_tokens,
    )
    return result.reshape(shape)


def solution(mesh):
    sizes = (mesh.shape["frames"], mesh.shape["rows"], mesh.shape["heads"])
    return jax.shard_map(
        functools.partial(body, sizes),
        mesh=mesh,
        in_specs=(
            P(("groups", "frames"), "rows", None, "heads"),
            P(),
            P(),
            P(None, "heads"),
            P(None, "heads"),
            P(None, "heads"),
            P("heads", None),
            P(("groups", "frames", "rows"), "heads"),
        ),
        out_specs=P(("groups", "frames"), "rows", None, "heads"),
        check_vma=False,
    )
```
